32 devices in a mesh: pairs: 2 (over x), band: 16 (over z, y, core).
Axes of the slice: x: 2, y: 2, z: 4, core: 2. Of those that a mesh axis runs over, the one named last changes fastest.
Arguments:
- query_tiles: bfloat16 [512, 256, 128], P(('pairs', 'band')), parts along dimension 0, may hold values from -52 to 52
- target: bfloat16 [512, 256, 128], P(('pairs', 'band')), parts along dimension 0, may hold values from -6 to 6
- tile_home: int32 [512], P('pairs'), parts along dimension 0, may hold values from 0 to 255, as said below
- candidates: int32 [512, 64], P(('pairs', 'band')), parts along dimension 0, may hold values from 0 to 255, as said below
- valid_mask: int32 [512, 64], P(('pairs', 'band')), parts along dimension 0, may hold values from 0 to 1, as said below
Outputs:
- matched: bfloat16 [512, 256, 128], P(('pairs', 'band')), parts along dimension 0
The draws below stay inside these ranges and needn't reach their ends.
There are 2 independent parts, one for each index of `pairs`. The reference program is written for one: setup_inputs(seed, part) draws one part's arguments, and reference() takes and returns one part's arrays. A program takes and returns all parts, laid end to end along the dimension named above; each array names one. Nothing has to cross between parts.
Inputs may be any that keep to these rules, and one draw needn't show every extreme that they name: `tile_home`: a permutation of 0 to 255; target tile ids that agree modulo 16 are stored on the same device, storage row r lying on device r // 16. Ids in a row are distinct; the candidates of one device's query tiles all lie in one run of 128 consecutive ids taken modulo 256, and its first two query tiles together name every id of that run. `valid_mask`: the first entry of every row is 1.
All inputs are finite; a program needn't handle non-finite values.
Results may differ from the reference program's by a relative error of at most 0.0034.
Values may be sent and summed in bfloat16 or wider, within the bound.
No kernel may reach another device: no remote copies, remote signals or barrier semaphores. Data moves between devices by JAX's collectives and lax.ppermute only.
A program may use at most 128 MiB of HBM per device.

```python
import math
import jax
import jax.numpy as jnp
from jax import lax

P_SIZE = 256
C = 128
K = 64
TILES_DEV = 16
NT = 256
WIN = 128
N_BAND = 16


def home_table(key):
    owner_order = jax.random.permutation(jax.random.fold_in(key, 201), N_BAND)
    slot_keys = jax.random.split(jax.random.fold_in(key, 202), N_BAND)
    slot_perms = jax.vmap(lambda subkey: jax.random.permutation(subkey, TILES_DEV))(slot_keys)
    tile_ids = jnp.arange(NT, dtype=jnp.int32)
    residue = tile_ids % N_BAND
    quotient = tile_ids // N_BAND
    return (owner_order[residue] * TILES_DEV + slot_perms[residue, quotient]).astype(jnp.int32)


def candidate_table(key):
    starts = jax.random.randint(jax.random.fold_in(key, 101), (N_BAND,), 0, NT)
    keys_all = jax.random.split(jax.random.fold_in(key, 102), N_BAND * TILES_DEV)
    perms = jax.vmap(lambda subkey: jax.random.permutation(subkey, WIN))(keys_all)
    perms = perms.reshape(N_BAND, TILES_DEV, WIN)
    positions = jnp.concatenate([perms[:, :1, :K], perms[:, :1, K:], perms[:, 2:, :K]], axis=1)
    ident = (starts[:, None, None] + positions) % NT
    return ident.reshape(NT, K).astype(jnp.int32)


def target_table(key):
    base = jnp.clip(jax.random.normal(jax.random.fold_in(key, 301), (NT, P_SIZE, C), jnp.float32), -6.0, 6.0)
    return base


def draw_tile_home(key, part):
    return home_table(key)


def draw_candidates(key, part):
    return candidate_table(key)


def draw_valid_mask(key, part):
    levels = jax.random.randint(jax.random.fold_in(key, 401), (NT, K), 0, 4)
    column = jnp.arange(K, dtype=jnp.int32)[None, :]
    return jnp.where(column == 0, 1, (levels > 0).astype(jnp.int32)).astype(jnp.int32)


def draw_target(key, part):
    return target_table(key).astype(jnp.bfloat16)


def draw_query_tiles(key, part):
    base = jnp.clip(jax.random.normal(jax.random.fold_in(key, 501), (NT, P_SIZE, C), jnp.float32), -6.0, 6.0)
    return base.astype(jnp.bfloat16)


def setup_inputs(seed: int = 0, part: int = 0) -> dict:
    key_of = jax.random.split(jax.random.key(seed), 6)
    own_keys = jax.random.split(jax.random.fold_in(key_of[5], part), 6)
    query_tiles = draw_query_tiles(jax.random.fold_in(jax.random.fold_in(key_of[5], part), 71), part)
    target = draw_target(jax.random.fold_in(jax.random.fold_in(key_of[5], part), 71), part)
    tile_home = draw_tile_home(jax.random.fold_in(jax.random.fold_in(key_of[5], part), 71), part)
    candidates = draw_candidates(jax.random.fold_in(jax.random.fold_in(key_of[5], part), 71), part)
    valid_mask = draw_valid_mask(jax.random.fold_in(jax.random.fold_in(key_of[5], part), 71), part)
    return dict(query_tiles=query_tiles, target=target, tile_home=tile_home, candidates=candidates, valid_mask=valid_mask)


def attend_tile(tile_query, tile_keys, keep_mask):
    per_tile = tile_keys.shape[0] // keep_mask.shape[0]
    scores = jnp.dot(tile_query, tile_keys.T, preferred_element_type=jnp.float32) * (1.0 / math.sqrt(tile_query.shape[1]))
    allowed = jnp.repeat(keep_mask > 0, per_tile)[None, :]
    scores = jnp.where(allowed, scores, -jnp.inf)
    peak = lax.optimization_barrier(jnp.max(scores, axis=1, keepdims=True))
    raised = jnp.exp(scores - peak)
    totals = lax.optimization_barrier(jnp.sum(raised, axis=1, keepdims=True))
    weights = (raised / totals).astype(jnp.bfloat16)
    return jnp.dot(weights, tile_keys, preferred_element_type=jnp.float32).astype(jnp.bfloat16)

def reference(query_tiles, target, tile_home, candidates, valid_mask):

    def one_tile(packed):
        tile_query, chosen, keep_mask = packed
        stored = target[tile_home[chosen]].reshape(-1, target.shape[2])
        return attend_tile(tile_query, stored, keep_mask)
    return lax.map(one_tile, (query_tiles, candidates, valid_mask))
```

```python
import functools
import math

import jax
import jax.numpy as jnp
from jax import lax
from jax.experimental import pallas as pl
from jax.experimental.pallas import tpu as pltpu
from jax.sharding import PartitionSpec as P


TARGET_ABS = 6.0
EXP_RANGE = 77.0
GROUP = 8
STEP = 2 * GROUP
SHIFT = 4096
NEG = -1e30


def matmul(a, b, ca, cb):
    return lax.dot_general(a, b, (((ca,), (cb,)), ((), ())), preferred_element_type=jnp.float32)


def stage_kernel(sizes, first, last, scale, counts, pairs, q_ref, *refs):
    chunks, refs = refs[: len(sizes)], refs[len(sizes) :]
    if not first:
        acc_in, sum_in, top_in, refs = *refs[:3], refs[3:]
    if last:
        out_ref, acc, total, top, scores, keys = refs
    else:
        acc, total, top, scores, keys = refs
    tiles = q_ref.shape[0]
    if first:
        acc[...] = jnp.zeros_like(acc)
        total[...] = jnp.zeros_like(total)
        top[...] = jnp.full_like(top, NEG)
    else:
        acc[...] = acc_in[...]
        total[...] = sum_in[...]
        top[...] = top_in[...]
    if len(sizes) == 1:
        key_at = lambda t: chunks[0][t]
    else:
        key_at = lambda t: keys[t]
        base = 0
        for size, chunk in zip(sizes, chunks):
            pltpu.sync_copy(chunk, keys.at[pl.ds(base, size)])
            base += size

    def split(code):
        row = code // SHIFT
        return row, jnp.minimum(row, tiles - 1), code % SHIFT

    def push(group, slot):
        for u in range(GROUP):
            _, qi, ki = split(pairs[group * GROUP + u])
            scores[slot, u] = matmul(key_at(ki), q_ref[qi], 1, 1)

    def pull(group, slot):
        for u in range(GROUP):
            row, _, ki = split(pairs[group * GROUP + u])
            raised = jnp.exp2(scores[slot, u] * scale)
            acc[row] += matmul(key_at(ki).T, raised.astype(jnp.bfloat16), 1, 0)
            total[row] += raised.reshape(-1, 8, raised.shape[1]).sum(0)

    push(0, 0)

    def body(j, carry):
        push(2 * j + 1, 1)
        pull(2 * j, 0)
        push(2 * j + 2, 0)
        pull(2 * j + 1, 1)
        return carry

    lax.fori_loop(0, counts[0], body, 0)

    def careful(j, carry):
        row, qi, ki = split(pairs[counts[0] * STEP + j])
        tile_keys = key_at(ki)
        scaled = matmul(tile_keys, q_ref[qi], 1, 1) * scale
        peak = jnp.maximum(top[row], jnp.max(scaled, axis=0, keepdims=True))
        fade = jnp.exp2(top[row] - peak)
        raised = jnp.exp2(scaled - peak[0:1])
        acc[row] = acc[row] * fade[0:1] + matmul(tile_keys.T, raised.astype(jnp.bfloat16), 1, 0)
        total[row] = total[row] * fade + raised.reshape(-1, 8, raised.shape[1]).sum(0)
        top[row] = peak
        return carry

    lax.fori_loop(0, counts[1], careful, 0)
    if last:

        def finish(i, carry):
            out_ref[i] = (acc[i] / jnp.sum(total[i], axis=0, keepdims=True)).T.astype(out_ref.dtype)
            return carry

        lax.fori_loop(0, tiles, finish, 0)


def run_stage(first, last, counts, pairs, query, chunks, state):
    tiles, pixels, channels = query.shape
    scale = math.log2(math.e) / math.sqrt(channels)
    sizes = tuple(c.shape[0] for c in chunks)
    shapes = [(tiles + 1, channels, pixels), (tiles + 1, 8, pixels), (tiles + 1, 8, pixels)]

    vmem = pl.BlockSpec(memory_space=pltpu.VMEM)
    smem = pl.BlockSpec(memory_space=pltpu.SMEM)
    state_types = [jax.ShapeDtypeStruct(s, jnp.float32) for s in shapes]
    scratch = [pltpu.VMEM((2, GROUP, pixels, pixels), jnp.float32)]
    chunk_spec = vmem if len(sizes) == 1 else pl.BlockSpec(memory_space=pl.ANY)
    key_rows = 1 if len(sizes) == 1 else sum(sizes)
    scratch.append(pltpu.VMEM((key_rows, pixels, channels), query.dtype))
    if last:
        scratch = [pltpu.VMEM(s, jnp.float32) for s in shapes] + scratch
        out_shape = jax.ShapeDtypeStruct(query.shape, query.dtype)
        out_specs = vmem
    else:
        out_shape, out_specs = state_types, [vmem] * 3
    work = tiles * sum(sizes) * 3 // 8 * pixels * pixels
    return pl.pallas_call(
        functools.partial(stage_kernel, sizes, first, last, scale),
        out_shape=out_shape,
        in_specs=[smem, smem, vmem] + [chunk_spec] * len(sizes) + [vmem] * (0 if first else 3),
        out_specs=out_specs,
        scratch_shapes=scratch,
        compiler_params=pltpu.CompilerParams(vmem_limit_bytes=60 * 1024 * 1024),
        cost_estimate=pl.CostEstimate(
            flops=4 * channels * work, transcendentals=work, bytes_accessed=sum(sizes) * pixels * channels * 2
        ),
    )(counts, pairs, query, *chunks, *(() if first else state))


def exclusive(counts, axis):
    n = counts.shape[axis]
    before = (jnp.arange(n)[:, None] < jnp.arange(n)[None, :]).astype(jnp.float32)
    return jnp.moveaxis(jnp.tensordot(counts, before, ((axis,), (0,)), precision=lax.Precision.HIGHEST), -1, axis)


def plan(query, rows, stage_of, key_of, valid, lengths):
    tiles, width = stage_of.shape
    spread = jnp.max(jnp.sum(jnp.abs(query.astype(jnp.float32)), axis=2), axis=1)
    careful = spread * (TARGET_ABS / math.sqrt(query.shape[2])) > EXP_RANGE
    number = len(lengths)
    member = (stage_of[None] == jnp.arange(number)[:, None, None]) & (valid[None] > 0)
    kinds = jnp.stack([member & ~careful[None, :, None], member & careful[None, :, None]]).astype(jnp.float32)
    in_row = exclusive(kinds, 3)
    row_sums = kinds.sum(3)
    rank = in_row + exclusive(row_sums, 2)[..., None]
    sums = row_sums.sum(2).astype(jnp.int32)
    steps = (sums[0] + STEP - 1) // STEP
    starts = [0]
    for length in lengths:
        starts.append(starts[-1] + length)
    offset = jnp.asarray(starts[:-1], jnp.int32)
    base = jnp.stack([offset, offset + steps * STEP])
    place = jnp.sum(jnp.where(kinds > 0, rank.astype(jnp.int32) + base[:, :, None, None] + 1, 0), axis=(0, 1))
    code = jnp.arange(tiles, dtype=jnp.int32)[:, None] * SHIFT + key_of
    blank = tiles * SHIFT
    hit = place.reshape(-1, 1) == jnp.arange(1, starts[-1] + 1, dtype=jnp.int32)[None, :]
    listed = jnp.sum(jnp.where(hit, (code - blank).reshape(-1, 1), 0), axis=0) + blank
    counts = jnp.stack([steps, sums[1]], axis=1)
    return [(counts[s], listed[starts[s] : starts[s + 1]]) for s in range(number)]


def pick(table, index):
    hit = index[..., None] == jnp.arange(table.shape[0], dtype=jnp.int32)
    return jnp.sum(jnp.where(hit, table, 0), axis=-1)


def list_length(tiles, width, key_tiles):
    return tiles * min(width, key_tiles) + 3 * STEP


def body(band, query, target, tile_home, candidates, valid):
    tiles, width = candidates.shape
    held = target.shape[0]
    rows = pick(tile_home, candidates)
    if band % 4 or band > 16 or held % 2:
        source = lax.all_gather(target, "band", axis=0, tiled=True)
        length = list_length(tiles, width, source.shape[0])
        ((counts, pairs),) = plan(query, rows, jnp.zeros_like(rows), rows, valid, [length])
        return run_stage(True, True, counts, pairs, query, [source], None)

    chips, side, half = band // 2, band // 4, held // 2

    def spot(chip):
        return jnp.where(chip % 2 == 0, chip // 2, chips - 1 - chip // 2)

    def chip_at(k):
        return 2 * k if k < side else 2 * (chips - 1 - k) + 1

    def hop(step):
        moves = []
        for k in range(chips):
            a, b = chip_at(k), chip_at((k + step) % chips)
            moves += [(2 * a + c, 2 * b + c) for c in range(2)]
        return moves

    across = [(i, i ^ 1) for i in range(band)]
    send = lambda x, moves: lax.ppermute(x, "band", moves)
    far = chips // 2

    ahead, back = target, target
    groups = [[target, send(target, across)]]
    for step in range(1, far + 1):
        if step == far:
            ahead, back = ahead[:half], back[half:]
        ahead, back = send(ahead, hop(1)), send(back, hop(-1))
        groups.append([ahead, back, send(ahead, across), send(back, across)])

    me = lax.axis_index("band")
    device, slot = rows // held, rows % held
    away = (spot(device // 2) - spot(me // 2)) % chips
    mine = (device % 2) == (me % 2)
    from_behind = away > far
    stage_of = jnp.where(from_behind, chips - away, away)
    near = jnp.where(mine, 0, 2 * held) + jnp.where(from_behind, 0, held) + slot
    edge = jnp.where(mine, 0, held) + slot
    key_of = jnp.where((away == 0) | (away == far), edge, near)
    lengths = [list_length(tiles, width, sum(c.shape[0] for c in g)) for g in groups]
    lists = plan(query, rows, stage_of, key_of, valid, lengths)
    state = None
    for s, (group, (counts, pairs)) in enumerate(zip(groups, lists)):
        state = run_stage(s == 0, s == far, counts, pairs, query, group, state)
    return state


def solution(mesh):
    in_specs = (
        P(("pairs", "band"), None, None),
        P(("pairs", "band"), None, None),
        P("pairs"),
        P(("pairs", "band"), None),
        P(("pairs", "band"), None),
    )
    out_specs = P(("pairs", "band"), None, None)
    return jax.shard_map(
        functools.partial(body, mesh.shape["band"]), mesh=mesh, in_specs=in_specs, out_specs=out_specs, check_vma=False
    )
```
